32 devices in a mesh: group: 4 (over y, x), dp: 2 (over core), tensor: 4 (over z).
Axes of the slice: x: 2, y: 2, z: 4, core: 2. Of those that a mesh axis runs over, the one named last changes fastest.
Arguments:
- tokens: bfloat16 [8192, 2048], P(('group', 'dp')), may hold values from -6 to 6
- norm_gain: bfloat16 [2048], replicated, may hold values from 0.099609375 to 1.8984375
- w_query: bfloat16 [2048, 2048], P(None, 'tensor'), may hold values from -0.25 to 0.25
- w_keyval: bfloat16 [2048, 512], P(None, 'tensor'), may hold values from -0.125 to 0.125
- w_out: bfloat16 [2048, 2048], P('tensor'), may hold values from -0.8984375 to 0.8984375
- kv_cache: bfloat16 [4, 32, 16, 128, 512], P(None, ('group', 'dp'), None, None, 'tensor'), may hold values from -400 to 400
- lengths: int32 [32, 2], P(('group', 'dp')), may hold values from 0 to 2048, as said below
- dest_slot: int32 [32, 16], replicated, may hold values from 0 to 511, as said below
Outputs:
- mixed: bfloat16 [8192, 2048], P(('group', 'dp', 'tensor'))
- decode_cache: bfloat16 [4, 512, 128, 512], P(None, ('group', 'dp'), None, 'tensor')
The draws below stay inside these ranges and needn't reach their ends.
Inputs may be any that keep to these rules, and one draw needn't show every extreme that they name: lengths[p, 0] lies in 0 to 2048 and lengths[p, 1] in 1 to 256; 2048 and 256 are each taken by some prompt; the prompts r * 4 to r * 4 + 3 of each index r of group and dp together hold exactly 32 live blocks. dest_slot is a permutation of the 512 slots; the slots of the index r of group and dp together are r * 4 * 16 onward; the blocks of prompts r * 4 to r * 4 + 3 send exactly 8 blocks to each index, of which exactly 4 is live.
All inputs are finite; a program needn't handle non-finite values.
Results may differ from the reference program's by a relative error of at most 0.009.
Values may be sent and summed in bfloat16 or wider, within the bound.
A program may use at most 128 MiB of HBM per device.

```python
import jax
import jax.numpy as jnp
from jax import lax

D = 2048
H = 32
HD = 64
KVH = 4
BLK = 128
NBW = 16
NEW = 256
LAYERS = 4
PR_DEV = 4
WIN = 2048
PROMPTS = 32
TOKENS = 8192
N_GROUP = 4
N_DP = 2


def draw_kv_cache(key, part):
    shape = (LAYERS, PROMPTS, NBW, BLK, KVH * 2 * HD)
    normal_vals = jnp.clip(jax.random.normal(jax.random.fold_in(key, 3), shape, jnp.float32), -6.0, 6.0)
    return normal_vals.astype(jnp.bfloat16)


def live_plan(key):
    base = jax.random.fold_in(key, 7)
    half = PROMPTS // 2
    first = jax.random.randint(jax.random.fold_in(base, 1), (half,), 0, NBW + 1)
    top_pair = jax.random.randint(jax.random.fold_in(base, 3), (), 0, half)
    first = jnp.where(jnp.arange(half) == top_pair, NBW, first)
    counts = jnp.stack([first, NBW - first], axis=1).reshape(PROMPTS)
    offset = jax.random.randint(jax.random.fold_in(base, 5), (PROMPTS,), 0, BLK)
    history = jnp.where(counts > 0, (counts - 1) * BLK + 1 + offset, 0)
    history = jnp.where(jnp.arange(PROMPTS) == 2 * top_pair, WIN, history)
    return (counts.astype(jnp.int32), history.astype(jnp.int32))


def draw_lengths(key, part):
    counts, history = live_plan(key)
    base = jax.random.fold_in(key, 9)
    fresh_len = jax.random.randint(jax.random.fold_in(base, 2), (PROMPTS,), 1, NEW + 1)
    top_new = jax.random.randint(jax.random.fold_in(base, 4), (), 0, PROMPTS)
    fresh_len = jnp.where(jnp.arange(PROMPTS) == top_new, NEW, fresh_len)
    return jnp.stack([history, fresh_len], axis=1).astype(jnp.int32)


def draw_dest_slot(key, part):
    counts, history = live_plan(key)
    devices = N_GROUP * N_DP
    per_dev = PR_DEV * NBW
    per_peer = per_dev // devices
    live = (jnp.arange(NBW)[None, :] >= NBW - counts[:, None]).astype(jnp.int32).reshape(devices, per_dev)
    base = jax.random.fold_in(key, 11)
    mix_keys = jax.random.split(jax.random.fold_in(base, 3), devices)
    mix = jax.vmap(lambda kk: jax.random.permutation(kk, per_dev))(mix_keys)
    score = (1 - live) * per_dev + mix
    order = jnp.argsort(score, axis=1, stable=True)
    position = jnp.argsort(order, axis=1, stable=True)
    shifts = jax.random.randint(jax.random.fold_in(base, 4), (devices, 1), 0, devices)
    receiver = (position + shifts) % devices
    within = position // devices
    recv_keys = jax.random.split(jax.random.fold_in(base, 2), devices)
    recv_perm = jax.vmap(lambda kk: jax.random.permutation(kk, per_dev))(recv_keys)
    senders = jnp.arange(devices)[:, None]
    slot_local = recv_perm[receiver, senders * per_peer + within]
    dest = receiver * per_dev + slot_local
    return dest.reshape(PROMPTS, NBW).astype(jnp.int32)


def level_of(stream_key, shape, shards, least, largest):
    def one(axis_at, shards_of):
        draws = jax.random.uniform(jax.random.fold_in(jax.random.fold_in(stream_key, 6), axis_at), (shards_of,), jnp.float32, least / len(shards), largest / len(shards))
        return jnp.repeat(jnp.exp(draws), shape[axis_at] // shards_of).reshape((-1,) + (1,) * (len(shape) - axis_at - 1))

    level = one(*shards[0])
    for cut in shards[1:]:
        level = level * one(*cut)
    return level


def centred(rng, extent, width, reach, pieces=(), kind=jnp.bfloat16):
    values = jax.random.normal(rng, extent, jnp.float32) * width
    if len(pieces) > 0:
        values = level_of(rng, extent, pieces, -0.22, 0.18) * values
    return jnp.clip(values, min=-reach, max=reach).astype(kind)


def setup_inputs(seed: int = 0) -> dict:
    key_list = jax.random.split(jax.random.key(seed), 9)
    tokens = centred(key_list[0], (TOKENS, D), 1.0, 6.0, ((0, 8),))
    norm_gain = jnp.clip(1.0 + 0.18 * jax.random.normal(key_list[1], (D,), jnp.float32), 0.099609375, 1.8984375).astype(jnp.bfloat16)
    w_query = centred(key_list[2], (D, H * HD), (D // 4) ** -0.5, 0.25, ((1, 4),))
    w_keyval = centred(key_list[3], (D, KVH * 2 * HD), D ** -0.5, 0.125, ((1, 4),))
    w_out = centred(key_list[4], (H * HD, D), 0.15, 0.8984375, ((0, 4),))
    kv_cache = draw_kv_cache(jax.random.fold_in(key_list[8], 71), 0)
    lengths = draw_lengths(jax.random.fold_in(key_list[8], 71), 0)
    dest_slot = draw_dest_slot(jax.random.fold_in(key_list[8], 71), 0)
    return dict(tokens=tokens, norm_gain=norm_gain, w_query=w_query, w_keyval=w_keyval, w_out=w_out, kv_cache=kv_cache, lengths=lengths, dest_slot=dest_slot)


def reference(tokens, norm_gain, w_query, w_keyval, w_out, kv_cache, lengths, dest_slot):
    tokens_f = tokens.astype(jnp.float32)
    normed = (tokens_f * lax.rsqrt(lax.optimization_barrier(jnp.mean(tokens_f * tokens_f, axis=-1, keepdims=True)) + 1e-05) * norm_gain.astype(jnp.float32)).astype(jnp.bfloat16)
    query = jnp.dot(normed, w_query, preferred_element_type=jnp.float32).astype(jnp.bfloat16)
    query = query.reshape(PROMPTS, NEW, KVH, H // KVH, HD)
    keyval = jnp.dot(normed, w_keyval, preferred_element_type=jnp.float32).astype(jnp.bfloat16)
    keyval = keyval.reshape(PROMPTS, NEW, KVH, 2, HD)
    cache = kv_cache[0].reshape(PROMPTS, WIN, KVH, 2, HD)
    scale = 1.0 / HD ** 0.5
    query_pos = jnp.arange(NEW)[:, None]
    key_pos = jnp.arange(WIN + NEW)[None, :]

    def attend(items):
        query_p, cache_p, fresh_p, history, fresh_len = items
        pairs = jnp.concatenate([cache_p, fresh_p], axis=0)
        keys_f = pairs[:, :, 0].astype(jnp.float32)
        vals_f = pairs[:, :, 1].astype(jnp.float32)
        scores = jnp.einsum('ckgd,tkd->kgct', query_p.astype(jnp.float32), keys_f) * scale
        visible = jnp.where(key_pos < WIN, (key_pos >= WIN - history) & (key_pos >= query_pos + 1), key_pos - WIN <= query_pos)
        scores = jnp.where(visible, scores, -1e+30)
        scores = scores - lax.optimization_barrier(jnp.max(scores, axis=-1, keepdims=True))
        expo = jnp.exp(scores)
        weights = (expo / lax.optimization_barrier(jnp.sum(expo, axis=-1, keepdims=True))).astype(jnp.bfloat16)
        mixed_p = jnp.einsum('kgct,tkd->ckgd', weights.astype(jnp.float32), vals_f)
        mixed_p = mixed_p.astype(jnp.bfloat16).reshape(NEW, H * HD)
        return jnp.where((jnp.arange(NEW) < fresh_len)[:, None], mixed_p, jnp.zeros_like(mixed_p))
    attn = lax.map(attend, (query, cache, keyval, lengths[:, 0], lengths[:, 1]))
    attn = attn.reshape(TOKENS, H * HD)
    mixed = jnp.dot(attn, w_out, preferred_element_type=jnp.float32).astype(jnp.bfloat16)
    live_mask = ((jnp.arange(NBW)[None, :] + 1) * BLK > WIN - lengths[:, 0:1]).astype(kv_cache.dtype)
    blocks = kv_cache * live_mask[None, :, :, None, None]
    blocks = blocks.reshape(LAYERS, PROMPTS * NBW, BLK, KVH * 2 * HD)
    decode_cache = jnp.zeros_like(blocks).at[:, dest_slot.reshape(-1).astype(jnp.int32)].set(blocks)
    return (mixed, decode_cache)
```

```python
import jax
import jax.numpy as jnp
from jax import lax
from jax.experimental import pallas as pl
from jax.experimental.pallas import tpu as pltpu
from jax.sharding import PartitionSpec as P

HD = 64
EPS = 1e-05
CHUNK = 256
NEG = -1e30
VMEM_LIMIT = 48 * 1024 * 1024


def project_kernel(tok_ref, gain_ref, wq_ref, wkv_ref, q_ref, kv_ref):
    x = tok_ref[...].astype(jnp.float32)
    inv = lax.rsqrt(jnp.mean(x * x, axis=-1, keepdims=True) + EPS)
    normed = (x * inv * gain_ref[...].astype(jnp.float32)).astype(jnp.bfloat16)
    kv_ref[...] = jnp.dot(normed, wkv_ref[...], preferred_element_type=jnp.float32).astype(
        jnp.bfloat16
    )
    q = jnp.dot(normed, wq_ref[...], preferred_element_type=jnp.float32) * (1.0 / HD**0.5)
    low = lax.broadcasted_iota(jnp.int32, (q.shape[0], 2 * HD), 1) < HD
    for pair in range(q.shape[1] // (2 * HD)):
        both = q[:, pair * 2 * HD : (pair + 1) * 2 * HD]
        q_ref[2 * pair] = jnp.where(low, both, 0.0).astype(jnp.bfloat16)
        q_ref[2 * pair + 1] = jnp.where(low, pltpu.roll(both, HD, 1), 0.0).astype(jnp.bfloat16)


def project(tokens, norm_gain, w_query, w_keyval, fresh_rows):
    rows, width = tokens.shape
    heads = w_query.shape[1] // HD
    return pl.pallas_call(
        project_kernel,
        grid=(rows // fresh_rows,),
        in_specs=[
            pl.BlockSpec((fresh_rows, width), lambda i: (i, 0)),
            pl.BlockSpec((1, width), lambda i: (0, 0)),
            pl.BlockSpec(w_query.shape, lambda i: (0, 0)),
            pl.BlockSpec(w_keyval.shape, lambda i: (0, 0)),
        ],
        out_specs=[
            pl.BlockSpec((heads, fresh_rows, 2 * HD), lambda i: (0, i, 0)),
            pl.BlockSpec((fresh_rows, 2 * HD), lambda i: (i, 0)),
        ],
        out_shape=[
            jax.ShapeDtypeStruct((heads, rows, 2 * HD), jnp.bfloat16),
            jax.ShapeDtypeStruct((rows, 2 * HD), jnp.bfloat16),
        ],
        compiler_params=pltpu.CompilerParams(vmem_limit_bytes=VMEM_LIMIT),
        cost_estimate=pl.CostEstimate(
            flops=2 * rows * width * (heads + 2) * HD, bytes_accessed=10**7, transcendentals=0
        ),
        name="project",
    )(tokens, norm_gain.reshape(1, width), w_query, w_keyval)


def attend_kernel(info_ref, q_ref, kv_ref, cache_ref, out_ref, s_ref, m_ref, acc_ref):
    history, fresh = info_ref[1], info_ref[2]
    heads, rows, lanes = q_ref.shape
    window = cache_ref.shape[2] * cache_ref.shape[3]
    chunks = window // CHUNK
    blocks = CHUNK // cache_ref.shape[3]
    start = window - history
    first = start // CHUNK
    trans = (((1,), (1,)), ((), ()))

    def cached(c):
        return cache_ref[0, 0, pl.ds(c * blocks, blocks)].reshape(CHUNK, lanes)

    def score(h, keys):
        return lax.dot_general(q_ref[h], keys, trans, preferred_element_type=jnp.float32)

    row = lax.broadcasted_iota(jnp.int32, (rows, CHUNK), 0)
    col = lax.broadcasted_iota(jnp.int32, (rows, CHUNK), 1)
    new = kv_ref[...]

    def keep(h, c, s, begin):
        s_ref[c, h] = s
        best = jnp.maximum(s[:, :lanes], s[:, lanes:])
        m_ref[h] = best if begin else jnp.maximum(m_ref[h], best)

    causal = col <= row
    for h in range(heads):
        keep(h, chunks, jnp.where(causal, score(h, new), NEG), True)

    @pl.when(first < chunks)
    def _():
        at = first * CHUNK + col
        seen = (at >= start) & (at >= row + 1)
        keys = cached(first)
        for h in range(heads):
            keep(h, first, jnp.where(seen, score(h, keys), NEG), False)

    def scores(c, carry):
        keys = cached(c)
        for h in range(heads):
            keep(h, c, score(h, keys), False)
        return carry

    lax.fori_loop(first + 1, chunks, scores, 0)

    for h in range(heads):
        m_ref[h] = jnp.broadcast_to(jnp.max(m_ref[h], axis=1, keepdims=True), (rows, lanes))

    low_keys = lax.broadcasted_iota(jnp.int32, (CHUNK, lanes), 1) < HD

    def gather(c, pairs, begin):
        vals = jnp.where(low_keys, jnp.ones_like(pairs), pairs)
        for h in range(heads):
            s = s_ref[c, h]
            m = m_ref[h]
            p = jnp.exp(s - jnp.concatenate([m, m], axis=1)).astype(jnp.bfloat16)
            o = jnp.dot(p, vals, preferred_element_type=jnp.float32)
            acc_ref[h] = o if begin else acc_ref[h] + o

    gather(chunks, new, True)

    def weigh(c, carry):
        gather(c, cached(c), False)
        return carry

    lax.fori_loop(first, chunks, weigh, 0)

    low = lax.broadcasted_iota(jnp.int32, (rows, lanes), 1) < HD
    live = lax.broadcasted_iota(jnp.int32, (rows, lanes), 0) < fresh
    for pair in range(heads // 2):
        even, odd = acc_ref[2 * pair], acc_ref[2 * pair + 1]
        even = pltpu.roll(even, HD, 1) / even
        odd = odd / pltpu.roll(odd, HD, 1)
        both = jnp.where(live, jnp.where(low, even, odd), 0.0)
        out_ref[:, pair * lanes : (pair + 1) * lanes] = both.astype(jnp.bfloat16)


def attend(info, query, keyval, kv_cache):
    heads, rows_all, lanes = query.shape
    _, prompts, blocks, block_len, _ = kv_cache.shape
    rows = rows_all // prompts
    chunks = blocks * block_len // CHUNK
    return pl.pallas_call(
        attend_kernel,
        grid_spec=pltpu.PrefetchScalarGridSpec(
            num_scalar_prefetch=1,
            grid=(1,),
            in_specs=[
                pl.BlockSpec((heads, rows, lanes), lambda i, info: (0, info[0], 0)),
                pl.BlockSpec((rows, lanes), lambda i, info: (info[0], 0)),
                pl.BlockSpec(
                    (1, 1, blocks, block_len, lanes), lambda i, info: (0, info[0], 0, 0, 0)
                ),
            ],
            out_specs=pl.BlockSpec((rows, heads * HD), lambda i, info: (0, 0)),
            scratch_shapes=[
                pltpu.VMEM((chunks + 1, heads, rows, CHUNK), jnp.float32),
                pltpu.VMEM((heads, rows, lanes), jnp.float32),
                pltpu.VMEM((heads, rows, lanes), jnp.float32),
            ],
        ),
        out_shape=jax.ShapeDtypeStruct((rows, heads * HD), jnp.bfloat16),
        compiler_params=pltpu.CompilerParams(vmem_limit_bytes=VMEM_LIMIT),
        cost_estimate=pl.CostEstimate(
            flops=10**9, bytes_accessed=10**6, transcendentals=0
        ),
        name="attend",
    )(info, query, keyval, kv_cache)


def pick_kernel(me_ref, dest_ref, len_ref, cache_ref, out_ref, count_ref, sems):
    per_dev = cache_ref.shape[1]
    total = out_ref.shape[0]
    blocks = per_dev // len_ref.shape[0]
    block_len = cache_ref.shape[2]
    window = blocks * block_len
    devices = count_ref.shape[0]
    capacity = total // devices
    base = me_ref[0] * per_dev
    for d in range(devices):
        count_ref[d] = 0

    def send(j, carry):
        p, b = j // blocks, j % blocks

        @pl.when((b + 1) * block_len > window - len_ref[p, 0])
        def _():
            peer = dest_ref[base + j] // per_dev
            at = peer * capacity + count_ref[peer]
            count_ref[peer] = count_ref[peer] + 1
            pltpu.make_async_copy(cache_ref.at[:, j], out_ref.at[at], sems.at[at]).start()

        return carry

    lax.fori_loop(0, per_dev, send, 0)

    def done(j, carry):
        pltpu.make_async_copy(cache_ref.at[:, 0], out_ref.at[j], sems.at[j]).wait()
        return carry

    lax.fori_loop(0, total, done, 0)


def place_kernel(src_ref, in_ref, out_ref, zero_ref, sems):
    zero_ref[...] = jnp.zeros_like(zero_ref)
    slots = out_ref.shape[1]

    def send(j, carry):
        src = src_ref[j]

        @pl.when(src >= 0)
        def _():
            pltpu.make_async_copy(in_ref.at[src], out_ref.at[:, j], sems.at[j]).start()

        @pl.when(src < 0)
        def _():
            pltpu.make_async_copy(zero_ref, out_ref.at[:, j], sems.at[j]).start()

        return carry

    lax.fori_loop(0, slots, send, 0)

    def done(j, carry):
        pltpu.make_async_copy(zero_ref, out_ref.at[:, j], sems.at[j]).wait()
        return carry

    lax.fori_loop(0, slots, done, 0)


def mix_kernel(a_ref, b_ref, c_ref, d_ref, order_ref, w_ref, out_ref):
    halves, shards, depth, _ = w_ref.shape
    total = None
    for ref, k in ((a_ref, 0), (b_ref, 1), (c_ref, 2), (d_ref, 3)):
        t = order_ref[k]
        for half in range(halves):
            term = jnp.dot(
                ref[:, half * depth : (half + 1) * depth],
                w_ref[half, t],
                preferred_element_type=jnp.float32,
            )
            total = term if total is None else total + term
    out_ref[...] = total.astype(jnp.bfloat16)


def mix(parts, order, w_all):
    rows, depth = parts[0].shape
    halves, shards, half_depth, width = w_all.shape
    tile = 512
    part = pl.BlockSpec((rows, depth), lambda i: (0, 0))
    return pl.pallas_call(
        mix_kernel,
        grid=(width // tile,),
        in_specs=[part] * len(parts)
        + [
            pl.BlockSpec(memory_space=pltpu.SMEM),
            pl.BlockSpec((halves, shards, half_depth, tile), lambda i: (0, 0, 0, i)),
        ],
        out_specs=pl.BlockSpec((rows, tile), lambda i: (0, i)),
        out_shape=jax.ShapeDtypeStruct((rows, width), jnp.bfloat16),
        compiler_params=pltpu.CompilerParams(vmem_limit_bytes=VMEM_LIMIT),
        cost_estimate=pl.CostEstimate(
            flops=2 * rows * depth * 4 * width, bytes_accessed=10**7, transcendentals=0
        ),
        name="mix",
    )(*parts, order, w_all)


def per_device(tokens, norm_gain, w_query, w_keyval, w_out, kv_cache, lengths, dest_slot):
    prompts = lengths.shape[0]
    fresh_rows = tokens.shape[0] // prompts
    layers, _, blocks_win, block_len, lane_width = kv_cache.shape
    window = blocks_win * block_len
    per_dev = prompts * blocks_win
    devices = lax.axis_size(("group", "dp"))
    capacity = per_dev // devices // 2
    total = devices * capacity
    me = lax.axis_index(("group", "dp")).astype(jnp.int32)
    dest_flat = dest_slot.reshape(-1)
    raw = kv_cache.reshape(layers, per_dev, block_len, lane_width)

    smem = pl.BlockSpec(memory_space=pltpu.SMEM)
    hbm = pl.BlockSpec(memory_space=pltpu.HBM)
    outgoing = pl.pallas_call(
        pick_kernel,
        in_specs=[smem, smem, smem, hbm],
        out_specs=hbm,
        out_shape=jax.ShapeDtypeStruct((total, layers, block_len, lane_width), jnp.bfloat16),
        scratch_shapes=[pltpu.SMEM((devices,), jnp.int32), pltpu.SemaphoreType.DMA((total,))],
        cost_estimate=pl.CostEstimate(flops=0, bytes_accessed=10**7, transcendentals=0),
        name="pick",
    )(me.reshape(1), dest_flat, lengths, raw)
    flat = jnp.zeros((8 * 128,), jnp.float32).at[: lengths.size].set(
        lengths.reshape(-1).astype(jnp.float32)
    )
    tiles = lax.all_gather(flat.reshape(8, 128), ("group", "dp"), axis=0)
    norm_gain, outgoing = lax.optimization_barrier((norm_gain, outgoing))
    incoming = lax.all_to_all(outgoing, ("group", "dp"), split_axis=0, concat_axis=0, tiled=True)

    cores = lax.axis_size("dp")
    depth = w_out.shape[0] // cores
    half = lax.dynamic_slice_in_dim(w_out, lax.axis_index("dp") * depth, depth, 0)
    w_all = lax.all_gather(half, ("dp", "tensor"), axis=0).reshape(cores, -1, *half.shape)

    query, keyval = project(tokens, norm_gain, w_query, w_keyval, fresh_rows)
    t_size = lax.axis_size("tensor")
    t = lax.axis_index("tensor").astype(jnp.int32)
    parts, order = [], []

    def shift(by):
        return [(i, (i + by) % t_size) for i in range(t_size)]

    for step in range(1, t_size + 1):
        p = (t + step) % t_size
        own = lax.dynamic_index_in_dim(lengths, p, 0, keepdims=False)
        info = jnp.concatenate([p.reshape(1), own])
        if step > 1:
            info = lax.optimization_barrier((info, part))[0]
        part = attend(info, query, keyval, kv_cache)
        parts.append(lax.ppermute(part, "tensor", shift(step)) if step < t_size else part)
        order.append((t - step + t_size) % t_size)
    mixed = mix(parts, jnp.stack(order), w_all)

    lengths_every = tiles.reshape(devices, -1)[:, : lengths.size].reshape(devices * prompts, -1)
    lengths_every = lengths_every.astype(jnp.int32)
    dest_all = dest_slot.reshape(devices, per_dev)
    recv_all = dest_all // per_dev
    live_all = (
        (jnp.arange(blocks_win)[None, :] + 1) * block_len > window - lengths_every[:, 0:1]
    ).reshape(devices, per_dev)
    same = recv_all[:, :, None] == recv_all[:, None, :]
    earlier = jnp.arange(per_dev)[None, :] < jnp.arange(per_dev)[:, None]
    rank = jnp.sum(same & earlier[None] & live_all[:, None, :], axis=2, dtype=jnp.int32)
    where_from = jnp.arange(devices, dtype=jnp.int32)[:, None] * capacity + rank
    slot = jnp.where((recv_all == me) & live_all, dest_all - me * per_dev, -1)
    hit = slot.reshape(1, -1) == jnp.arange(per_dev, dtype=jnp.int32)[:, None]
    source = jnp.max(jnp.where(hit, where_from.reshape(1, -1), -1), axis=1)
    decode_cache = pl.pallas_call(
        place_kernel,
        in_specs=[smem, hbm],
        out_specs=hbm,
        out_shape=jax.ShapeDtypeStruct((layers, per_dev, block_len, lane_width), jnp.bfloat16),
        scratch_shapes=[
            pltpu.VMEM((layers, block_len, lane_width), jnp.bfloat16),
            pltpu.SemaphoreType.DMA((per_dev,)),
        ],
        cost_estimate=pl.CostEstimate(flops=0, bytes_accessed=10**7, transcendentals=0),
        name="place",
    )(*lax.optimization_barrier((source, incoming, part))[:2])
    return (mixed, decode_cache)


def solution(mesh):
    in_specs = (
        P(("group", "dp"), None),
        P(),
        P(None, "tensor"),
        P(None, "tensor"),
        P("tensor", None),
        P(None, ("group", "dp"), None, None, "tensor"),
        P(("group", "dp"), None),
        P(),
    )
    out_specs = (P(("group", "dp", "tensor"), None), P(None, ("group", "dp"), None, "tensor"))
    return jax.shard_map(
        per_device, mesh=mesh, in_specs=in_specs, out_specs=out_specs, check_vma=False
    )
```

```python
import jax
import jax.numpy as jnp
from jax import lax
from jax.experimental import pallas as pl
from jax.experimental.pallas import tpu as pltpu
from jax.sharding import PartitionSpec as P

HD = 64
EPS = 1e-05
CHUNK = 256
NEG = -1e30
VMEM_LIMIT = 48 * 1024 * 1024


def project_kernel(tok_ref, gain_ref, wq_ref, wkv_ref, q_ref, kv_ref):
    x = tok_ref[...].astype(jnp.float32)
    inv = lax.rsqrt(jnp.mean(x * x, axis=-1, keepdims=True) + EPS)
    normed = (x * inv * gain_ref[...].astype(jnp.float32)).astype(jnp.bfloat16)
    kv_ref[...] = jnp.dot(normed, wkv_ref[...], preferred_element_type=jnp.float32).astype(
        jnp.bfloat16
    )
    q = jnp.dot(normed, wq_ref[...], preferred_element_type=jnp.float32) * (1.0 / HD**0.5)
    low = lax.broadcasted_iota(jnp.int32, (q.shape[0], 2 * HD), 1) < HD
    for pair in range(q.shape[1] // (2 * HD)):
        both = q[:, pair * 2 * HD : (pair + 1) * 2 * HD]
        q_ref[2 * pair] = jnp.where(low, both, 0.0).astype(jnp.bfloat16)
        q_ref[2 * pair + 1] = jnp.where(low, pltpu.roll(both, HD, 1), 0.0).astype(jnp.bfloat16)


def project(tokens, norm_gain, w_query, w_keyval, fresh_rows):
    rows, width = tokens.shape
    heads = w_query.shape[1] // HD
    return pl.pallas_call(
        project_kernel,
        grid=(rows // fresh_rows,),
        in_specs=[
            pl.BlockSpec((fresh_rows, width), lambda i: (i, 0)),
            pl.BlockSpec((1, width), lambda i: (0, 0)),
            pl.BlockSpec(w_query.shape, lambda i: (0, 0)),
            pl.BlockSpec(w_keyval.shape, lambda i: (0, 0)),
        ],
        out_specs=[
            pl.BlockSpec((heads, fresh_rows, 2 * HD), lambda i: (0, i, 0)),
            pl.BlockSpec((fresh_rows, 2 * HD), lambda i: (i, 0)),
        ],
        out_shape=[
            jax.ShapeDtypeStruct((heads, rows, 2 * HD), jnp.bfloat16),
            jax.ShapeDtypeStruct((rows, 2 * HD), jnp.bfloat16),
        ],
        compiler_params=pltpu.CompilerParams(vmem_limit_bytes=VMEM_LIMIT),
        cost_estimate=pl.CostEstimate(
            flops=2 * rows * width * (heads + 2) * HD, bytes_accessed=10**7, transcendentals=0
        ),
        name="project",
    )(tokens, norm_gain.reshape(1, width), w_query, w_keyval)


def attend_kernel(info_ref, q_ref, kv_ref, cache_ref, out_ref, s_ref, m_ref, l_ref, acc_ref):
    history, fresh = info_ref[1], info_ref[2]
    heads, rows, lanes = q_ref.shape
    window = cache_ref.shape[2] * cache_ref.shape[3]
    chunks = window // CHUNK
    blocks = CHUNK // cache_ref.shape[3]
    start = window - history
    first = start // CHUNK
    trans = (((1,), (1,)), ((), ()))

    def cached(c):
        return cache_ref[0, 0, pl.ds(c * blocks, blocks)].reshape(CHUNK, lanes)

    def score(h, keys):
        return lax.dot_general(q_ref[h], keys, trans, preferred_element_type=jnp.float32)

    row = lax.broadcasted_iota(jnp.int32, (rows, CHUNK), 0)
    col = lax.broadcasted_iota(jnp.int32, (rows, CHUNK), 1)
    new = kv_ref[...]

    def keep(h, c, s, begin):
        s_ref[c, h] = s
        best = jnp.maximum(s[:, :lanes], s[:, lanes:])
        m_ref[h] = best if begin else jnp.maximum(m_ref[h], best)

    causal = col <= row
    for h in range(heads):
        keep(h, chunks, jnp.where(causal, score(h, new), NEG), True)

    @pl.when(first < chunks)
    def _():
        at = first * CHUNK + col
        seen = (at >= start) & (at >= row + 1)
        keys = cached(first)
        for h in range(heads):
            keep(h, first, jnp.where(seen, score(h, keys), NEG), False)

    def scores(c, carry):
        keys = cached(c)
        for h in range(heads):
            keep(h, c, score(h, keys), False)
        return carry

    lax.fori_loop(first + 1, chunks, scores, 0)

    for h in range(heads):
        m_ref[h] = jnp.broadcast_to(jnp.max(m_ref[h], axis=1, keepdims=True), (rows, lanes))

    def exps(c, begin):
        for h in range(heads):
            m = m_ref[h]
            e = jnp.exp(s_ref[c, h] - jnp.concatenate([m, m], axis=1))
            s_ref[c, h] = e
            both = e[:, :lanes] + e[:, lanes:]
            l_ref[h] = both if begin else l_ref[h] + both

    def gather(c, pairs, begin):
        for h in range(heads):
            inv = l_ref[h]
            w = (s_ref[c, h] * jnp.concatenate([inv, inv], axis=1)).astype(jnp.bfloat16)
            o = jnp.dot(w, pairs, preferred_element_type=jnp.float32)
            acc_ref[h] = o if begin else acc_ref[h] + o

    exps(chunks, True)

    def exponentiate(c, carry):
        exps(c, False)
        return carry

    lax.fori_loop(first, chunks, exponentiate, 0)

    for h in range(heads):
        total = jnp.sum(l_ref[h], axis=1, keepdims=True)
        l_ref[h] = jnp.broadcast_to(1.0 / total, (rows, lanes))

    gather(chunks, new, True)

    def weigh(c, carry):
        gather(c, cached(c), False)
        return carry

    lax.fori_loop(first, chunks, weigh, 0)

    low = lax.broadcasted_iota(jnp.int32, (rows, lanes), 1) < HD
    live = lax.broadcasted_iota(jnp.int32, (rows, lanes), 0) < fresh
    for pair in range(heads // 2):
        even, odd = acc_ref[2 * pair], acc_ref[2 * pair + 1]
        even = pltpu.roll(even, HD, 1)
        both = jnp.where(live, jnp.where(low, even, odd), 0.0)
        out_ref[:, pair * lanes : (pair + 1) * lanes] = both.astype(jnp.bfloat16)


def attend(info, query, keyval, kv_cache):
    heads, rows_all, lanes = query.shape
    _, prompts, blocks, block_len, _ = kv_cache.shape
    rows = rows_all // prompts
    chunks = blocks * block_len // CHUNK
    return pl.pallas_call(
        attend_kernel,
        grid_spec=pltpu.PrefetchScalarGridSpec(
            num_scalar_prefetch=1,
            grid=(1,),
            in_specs=[
                pl.BlockSpec((heads, rows, lanes), lambda i, info: (0, info[0], 0)),
                pl.BlockSpec((rows, lanes), lambda i, info: (info[0], 0)),
                pl.BlockSpec(
                    (1, 1, blocks, block_len, lanes), lambda i, info: (0, info[0], 0, 0, 0)
                ),
            ],
            out_specs=pl.BlockSpec((rows, heads * HD), lambda i, info: (0, 0)),
            scratch_shapes=[
                pltpu.VMEM((chunks + 1, heads, rows, CHUNK), jnp.float32),
                pltpu.VMEM((heads, rows, lanes), jnp.float32),
                pltpu.VMEM((heads, rows, lanes), jnp.float32),
                pltpu.VMEM((heads, rows, lanes), jnp.float32),
            ],
        ),
        out_shape=jax.ShapeDtypeStruct((rows, heads * HD), jnp.bfloat16),
        compiler_params=pltpu.CompilerParams(vmem_limit_bytes=VMEM_LIMIT),
        cost_estimate=pl.CostEstimate(
            flops=10**9, bytes_accessed=10**6, transcendentals=0
        ),
        name="attend",
    )(info, query, keyval, kv_cache)


def pick_kernel(me_ref, dest_ref, len_ref, cache_ref, out_ref, count_ref, sems):
    layers, per_dev, block_len, lanes = cache_ref.shape
    total, rows, _ = out_ref.shape
    blocks = per_dev // len_ref.shape[0]
    window = blocks * block_len
    devices = count_ref.shape[0]
    capacity = total // devices
    base = me_ref[0] * per_dev
    tail = layers * block_len
    for d in range(devices):
        count_ref[d] = 0

    def block(j, at, l):
        return pltpu.make_async_copy(
            cache_ref.at[l, j], out_ref.at[at, pl.ds(l * block_len, block_len)], sems.at[at, l]
        )

    def send(j, carry):
        p, b = j // blocks, j % blocks

        @pl.when((b + 1) * block_len > window - len_ref[p, 0])
        def _():
            dest = dest_ref[base + j]
            peer = dest // per_dev
            at = peer * capacity + count_ref[peer]
            count_ref[peer] = count_ref[peer] + 1
            for l in range(layers):
                block(j, at, l).start()
            slot = jnp.full((rows - tail, lanes), dest - peer * per_dev, jnp.int32)
            out_ref[at, pl.ds(tail, rows - tail)] = slot.astype(jnp.float32).astype(jnp.bfloat16)

        return carry

    lax.fori_loop(0, per_dev, send, 0)

    def done(j, carry):
        for l in range(layers):
            block(0, j, l).wait()
        return carry

    lax.fori_loop(0, total, done, 0)


def place_kernel(slot_ref, in_ref, out_ref, src_ref, zero_ref, held_ref, in_sem, sems):
    total, _, _ = in_ref.shape
    layers, slots, block_len, _ = out_ref.shape
    load = pltpu.make_async_copy(in_ref, held_ref, in_sem)
    load.start()
    zero_ref[...] = jnp.zeros_like(zero_ref)

    def clear(j, carry):
        src_ref[j] = -1
        return carry

    lax.fori_loop(0, slots, clear, 0)

    def note(j, carry):
        src_ref[slot_ref[j]] = j
        return carry

    lax.fori_loop(0, total, note, 0)

    def fill(j, carry):
        @pl.when(src_ref[j] < 0)
        def _():
            for l in range(layers):
                pltpu.make_async_copy(zero_ref, out_ref.at[l, j], sems.at[l, j]).start()

        return carry

    lax.fori_loop(0, slots, fill, 0)
    load.wait()

    def send(j, carry):
        for l in range(layers):
            held = held_ref.at[j, pl.ds(l * block_len, block_len)]
            slot = slot_ref[j]
            pltpu.make_async_copy(held, out_ref.at[l, slot], sems.at[l, slot]).start()
        return carry

    lax.fori_loop(0, total, send, 0)

    def done(j, carry):
        for l in range(layers):
            pltpu.make_async_copy(zero_ref, out_ref.at[l, j], sems.at[l, j]).wait()
        return carry

    lax.fori_loop(0, slots, done, 0)


def mix_kernel(a_ref, b_ref, c_ref, d_ref, order_ref, w_ref, out_ref):
    halves, shards, depth, _ = w_ref.shape
    total = None
    for ref, k in ((a_ref, 0), (b_ref, 1), (c_ref, 2), (d_ref, 3)):
        t = order_ref[k]
        for half in range(halves):
            term = jnp.dot(
                ref[:, half * depth : (half + 1) * depth],
                w_ref[half, t],
                preferred_element_type=jnp.float32,
            )
            total = term if total is None else total + term
    out_ref[...] = total.astype(jnp.bfloat16)


def mix(parts, order, w_all):
    rows, depth = parts[0].shape
    halves, shards, half_depth, width = w_all.shape
    tile = 512
    part = pl.BlockSpec((rows, depth), lambda i: (0, 0))
    return pl.pallas_call(
        mix_kernel,
        grid=(width // tile,),
        in_specs=[part] * len(parts)
        + [
            pl.BlockSpec(memory_space=pltpu.SMEM),
            pl.BlockSpec((halves, shards, half_depth, tile), lambda i: (0, 0, 0, i)),
        ],
        out_specs=pl.BlockSpec((rows, tile), lambda i: (0, i)),
        out_shape=jax.ShapeDtypeStruct((rows, width), jnp.bfloat16),
        compiler_params=pltpu.CompilerParams(vmem_limit_bytes=VMEM_LIMIT),
        cost_estimate=pl.CostEstimate(
            flops=2 * rows * depth * 4 * width, bytes_accessed=10**7, transcendentals=0
        ),
        name="mix",
    )(*parts, order, w_all)


def per_device(tokens, norm_gain, w_query, w_keyval, w_out, kv_cache, lengths, dest_slot):
    prompts = lengths.shape[0]
    fresh_rows = tokens.shape[0] // prompts
    layers, _, blocks_win, block_len, lane_width = kv_cache.shape
    per_dev = prompts * blocks_win
    devices = lax.axis_size(("group", "dp"))
    capacity = per_dev // devices // 2
    total = devices * capacity
    me = lax.axis_index(("group", "dp")).astype(jnp.int32)
    dest_flat = dest_slot.reshape(-1)
    raw = kv_cache.reshape(layers, per_dev, block_len, lane_width)

    smem = pl.BlockSpec(memory_space=pltpu.SMEM)
    hbm = pl.BlockSpec(memory_space=pltpu.HBM)
    rows = layers * block_len + 16
    outgoing = pl.pallas_call(
        pick_kernel,
        in_specs=[smem, smem, smem, hbm],
        out_specs=pl.BlockSpec(memory_space=pltpu.VMEM),
        out_shape=jax.ShapeDtypeStruct((total, rows, lane_width), jnp.bfloat16),
        scratch_shapes=[
            pltpu.SMEM((devices,), jnp.int32),
            pltpu.SemaphoreType.DMA((total, layers)),
        ],
        compiler_params=pltpu.CompilerParams(vmem_limit_bytes=VMEM_LIMIT),
        cost_estimate=pl.CostEstimate(flops=0, bytes_accessed=10**7, transcendentals=0),
        name="pick",
    )(me.reshape(1), dest_flat, lengths, raw)
    norm_gain, outgoing = lax.optimization_barrier((norm_gain, outgoing))
    incoming = lax.all_to_all(outgoing, ("group", "dp"), split_axis=0, concat_axis=0, tiled=True)

    cores = lax.axis_size("dp")
    depth = w_out.shape[0] // cores
    half = lax.dynamic_slice_in_dim(w_out, lax.axis_index("dp") * depth, depth, 0)
    w_all = lax.all_gather(half, ("dp", "tensor"), axis=0).reshape(cores, -1, *half.shape)

    query, keyval = project(tokens, norm_gain, w_query, w_keyval, fresh_rows)
    t_size = lax.axis_size("tensor")
    t = lax.axis_index("tensor").astype(jnp.int32)
    parts, order = [], []

    def shift(by):
        return [(i, (i + by) % t_size) for i in range(t_size)]

    for step in range(1, t_size + 1):
        p = (t + step) % t_size
        own = lax.dynamic_index_in_dim(lengths, p, 0, keepdims=False)
        info = jnp.concatenate([p.reshape(1), own])
        if step > 1:
            info = lax.optimization_barrier((info, part))[0]
        part = attend(info, query, keyval, kv_cache)
        parts.append(lax.ppermute(part, "tensor", shift(step)) if step < t_size else part)
        order.append((t - step + t_size) % t_size)
    mixed = mix(parts, jnp.stack(order), w_all)

    slots = incoming[:, layers * block_len, 0].astype(jnp.int32)
    decode_cache = pl.pallas_call(
        place_kernel,
        in_specs=[smem, hbm],
        out_specs=hbm,
        out_shape=jax.ShapeDtypeStruct((layers, per_dev, block_len, lane_width), jnp.bfloat16),
        scratch_shapes=[
            pltpu.SMEM((per_dev,), jnp.int32),
            pltpu.VMEM((block_len, lane_width), jnp.bfloat16),
            pltpu.VMEM((total, rows, lane_width), jnp.bfloat16),
            pltpu.SemaphoreType.DMA,
            pltpu.SemaphoreType.DMA((layers, per_dev)),
        ],
        compiler_params=pltpu.CompilerParams(vmem_limit_bytes=VMEM_LIMIT),
        cost_estimate=pl.CostEstimate(flops=0, bytes_accessed=10**7, transcendentals=0),
        name="place",
    )(slots, lax.optimization_barrier((incoming, part))[0])
    return (mixed, decode_cache)


def solution(mesh):
    in_specs = (
        P(("group", "dp"), None),
        P(),
        P(None, "tensor"),
        P(None, "tensor"),
        P("tensor", None),
        P(None, ("group", "dp"), None, None, "tensor"),
        P(("group", "dp"), None),
        P(),
    )
    out_specs = (P(("group", "dp", "tensor"), None), P(None, ("group", "dp"), None, "tensor"))
    return jax.shard_map(
        per_device, mesh=mesh, in_specs=in_specs, out_specs=out_specs, check_vma=False
    )
```

```python
import functools

import jax
import jax.numpy as jnp
from jax import lax
from jax.experimental import pallas as pl
from jax.experimental.pallas import tpu as pltpu
from jax.sharding import PartitionSpec as P

HD = 64
EPS = 1e-05
CHUNK = 256
NEG = -1e30
VMEM_LIMIT = 48 * 1024 * 1024


def project_kernel(tok_ref, gain_ref, wq_ref, wkv_ref, q_ref, kv_ref):
    x = tok_ref[...].astype(jnp.float32)
    inv = lax.rsqrt(jnp.mean(x * x, axis=-1, keepdims=True) + EPS)
    normed = (x * inv * gain_ref[...].astype(jnp.float32)).astype(jnp.bfloat16)
    kv_ref[...] = jnp.dot(normed, wkv_ref[...], preferred_element_type=jnp.float32).astype(
        jnp.bfloat16
    )
    q = jnp.dot(normed, wq_ref[...], preferred_element_type=jnp.float32) * (1.0 / HD**0.5)
    low = lax.broadcasted_iota(jnp.int32, (q.shape[0], 2 * HD), 1) < HD
    for pair in range(q.shape[1] // (2 * HD)):
        both = q[:, pair * 2 * HD : (pair + 1) * 2 * HD]
        q_ref[2 * pair] = jnp.where(low, both, 0.0).astype(jnp.bfloat16)
        q_ref[2 * pair + 1] = jnp.where(low, pltpu.roll(both, HD, 1), 0.0).astype(jnp.bfloat16)


def project(tokens, norm_gain, w_query, w_keyval, fresh_rows):
    rows, width = tokens.shape
    heads = w_query.shape[1] // HD
    return pl.pallas_call(
        project_kernel,
        grid=(rows // fresh_rows,),
        in_specs=[
            pl.BlockSpec((fresh_rows, width), lambda i: (i, 0)),
            pl.BlockSpec((1, width), lambda i: (0, 0)),
            pl.BlockSpec(w_query.shape, lambda i: (0, 0)),
            pl.BlockSpec(w_keyval.shape, lambda i: (0, 0)),
        ],
        out_specs=[
            pl.BlockSpec((heads, fresh_rows, 2 * HD), lambda i: (0, i, 0)),
            pl.BlockSpec((fresh_rows, 2 * HD), lambda i: (i, 0)),
        ],
        out_shape=[
            jax.ShapeDtypeStruct((heads, rows, 2 * HD), jnp.bfloat16),
            jax.ShapeDtypeStruct((rows, 2 * HD), jnp.bfloat16),
        ],
        compiler_params=pltpu.CompilerParams(vmem_limit_bytes=VMEM_LIMIT),
        cost_estimate=pl.CostEstimate(
            flops=2 * rows * width * (heads + 2) * HD, bytes_accessed=10**7, transcendentals=0
        ),
        name="project",
    )(tokens, norm_gain.reshape(1, width), w_query, w_keyval)


def attend_kernel(info_ref, q_ref, kv_ref, cache_ref, out_ref, s_ref, m_ref, l_ref, acc_ref):
    history, fresh = info_ref[1], info_ref[2]
    heads, rows, lanes = q_ref.shape
    window = cache_ref.shape[2] * cache_ref.shape[3]
    chunks = window // CHUNK
    blocks = CHUNK // cache_ref.shape[3]
    start = window - history
    first = start // CHUNK
    trans = (((1,), (1,)), ((), ()))

    def cached(c):
        return cache_ref[0, 0, pl.ds(c * blocks, blocks)].reshape(CHUNK, lanes)

    def score(h, keys):
        return lax.dot_general(q_ref[h], keys, trans, preferred_element_type=jnp.float32)

    row = lax.broadcasted_iota(jnp.int32, (rows, CHUNK), 0)
    col = lax.broadcasted_iota(jnp.int32, (rows, CHUNK), 1)
    new = kv_ref[...]

    def keep(h, c, s, begin):
        s_ref[c, h] = s
        best = jnp.maximum(s[:, :lanes], s[:, lanes:])
        m_ref[h] = best if begin else jnp.maximum(m_ref[h], best)

    causal = col <= row
    for h in range(heads):
        keep(h, chunks, jnp.where(causal, score(h, new), NEG), True)

    @pl.when(first < chunks)
    def _():
        at = first * CHUNK + col
        seen = (at >= start) & (at >= row + 1)
        keys = cached(first)
        for h in range(heads):
            keep(h, first, jnp.where(seen, score(h, keys), NEG), False)

    def scores(c, carry):
        keys = cached(c)
        for h in range(heads):
            keep(h, c, score(h, keys), False)
        return carry

    lax.fori_loop(first + 1, chunks, scores, 0)

    for h in range(heads):
        m_ref[h] = jnp.broadcast_to(jnp.max(m_ref[h], axis=1, keepdims=True), (rows, lanes))

    def exps(c, begin):
        for h in range(heads):
            m = m_ref[h]
            e = jnp.exp(s_ref[c, h] - jnp.concatenate([m, m], axis=1))
            s_ref[c, h] = e
            both = e[:, :lanes] + e[:, lanes:]
            l_ref[h] = both if begin else l_ref[h] + both

    def gather(c, pairs, begin):
        for h in range(heads):
            inv = l_ref[h]
            w = (s_ref[c, h] * jnp.concatenate([inv, inv], axis=1)).astype(jnp.bfloat16)
            o = jnp.dot(w, pairs, preferred_element_type=jnp.float32)
            acc_ref[h] = o if begin else acc_ref[h] + o

    exps(chunks, True)

    def exponentiate(c, carry):
        exps(c, False)
        return carry

    lax.fori_loop(first, chunks, exponentiate, 0)

    for h in range(heads):
        total = jnp.sum(l_ref[h], axis=1, keepdims=True)
        l_ref[h] = jnp.broadcast_to(1.0 / total, (rows, lanes))

    gather(chunks, new, True)

    def weigh(c, carry):
        gather(c, cached(c), False)
        return carry

    lax.fori_loop(first, chunks, weigh, 0)

    low = lax.broadcasted_iota(jnp.int32, (rows, lanes), 1) < HD
    live = lax.broadcasted_iota(jnp.int32, (rows, lanes), 0) < fresh
    for pair in range(heads // 2):
        even, odd = acc_ref[2 * pair], acc_ref[2 * pair + 1]
        even = pltpu.roll(even, HD, 1)
        both = jnp.where(live, jnp.where(low, even, odd), 0.0)
        out_ref[:, pair * lanes : (pair + 1) * lanes] = both.astype(jnp.bfloat16)


def attend(info, query, keyval, kv_cache):
    heads, rows_all, lanes = query.shape
    _, prompts, blocks, block_len, _ = kv_cache.shape
    rows = rows_all // prompts
    chunks = blocks * block_len // CHUNK
    return pl.pallas_call(
        attend_kernel,
        grid_spec=pltpu.PrefetchScalarGridSpec(
            num_scalar_prefetch=1,
            grid=(1,),
            in_specs=[
                pl.BlockSpec((heads, rows, lanes), lambda i, info: (0, info[0], 0)),
                pl.BlockSpec((rows, lanes), lambda i, info: (info[0], 0)),
                pl.BlockSpec(
                    (1, 1, blocks, block_len, lanes), lambda i, info: (0, info[0], 0, 0, 0)
                ),
            ],
            out_specs=pl.BlockSpec((rows, heads * HD), lambda i, info: (0, 0)),
            scratch_shapes=[
                pltpu.VMEM((chunks + 1, heads, rows, CHUNK), jnp.float32),
                pltpu.VMEM((heads, rows, lanes), jnp.float32),
                pltpu.VMEM((heads, rows, lanes), jnp.float32),
                pltpu.VMEM((heads, rows, lanes), jnp.float32),
            ],
        ),
        out_shape=jax.ShapeDtypeStruct((rows, heads * HD), jnp.bfloat16),
        compiler_params=pltpu.CompilerParams(vmem_limit_bytes=VMEM_LIMIT),
        cost_estimate=pl.CostEstimate(
            flops=10**9, bytes_accessed=10**6, transcendentals=0
        ),
        name="attend",
    )(info, query, keyval, kv_cache)


def pick_kernel(me_ref, dest_ref, len_ref, cache_ref, out_ref, count_ref, sems):
    layers, per_dev, block_len, lanes = cache_ref.shape
    total, rows, _ = out_ref.shape
    blocks = per_dev // len_ref.shape[0]
    window = blocks * block_len
    devices = count_ref.shape[0]
    capacity = total // devices
    base = me_ref[0] * per_dev
    tail = layers * block_len
    for d in range(devices):
        count_ref[d] = 0

    def block(j, at, l):
        return pltpu.make_async_copy(
            cache_ref.at[l, j], out_ref.at[at, pl.ds(l * block_len, block_len)], sems.at[at, l]
        )

    def send(j, carry):
        p, b = j // blocks, j % blocks

        @pl.when((b + 1) * block_len > window - len_ref[p, 0])
        def _():
            dest = dest_ref[base + j]
            peer = dest // per_dev
            at = peer * capacity + count_ref[peer]
            count_ref[peer] = count_ref[peer] + 1
            for l in range(layers):
                block(j, at, l).start()
            slot = jnp.full((rows - tail, lanes), dest - peer * per_dev, jnp.int32)
            out_ref[at, pl.ds(tail, rows - tail)] = slot.astype(jnp.float32).astype(jnp.bfloat16)

        return carry

    lax.fori_loop(0, per_dev, send, 0)

    def done(j, carry):
        for l in range(layers):
            block(0, j, l).wait()
        return carry

    lax.fori_loop(0, total, done, 0)


def place_kernel(slot_ref, in_ref, out_ref, src_ref, zero_ref, held_ref, in_sem, sems):
    total, _, _ = in_ref.shape
    layers, slots, block_len, _ = out_ref.shape
    load = pltpu.make_async_copy(in_ref, held_ref, in_sem)
    load.start()
    zero_ref[...] = jnp.zeros_like(zero_ref)

    def clear(j, carry):
        src_ref[j] = -1
        return carry

    lax.fori_loop(0, slots, clear, 0)

    def note(j, carry):
        src_ref[slot_ref[j]] = j
        return carry

    lax.fori_loop(0, total, note, 0)

    def fill(j, carry):
        @pl.when(src_ref[j] < 0)
        def _():
            for l in range(layers):
                pltpu.make_async_copy(zero_ref, out_ref.at[l, j], sems.at[l, j]).start()

        return carry

    lax.fori_loop(0, slots, fill, 0)
    load.wait()

    def send(j, carry):
        for l in range(layers):
            held = held_ref.at[j, pl.ds(l * block_len, block_len)]
            slot = slot_ref[j]
            pltpu.make_async_copy(held, out_ref.at[l, slot], sems.at[l, slot]).start()
        return carry

    lax.fori_loop(0, total, send, 0)

    def done(j, carry):
        for l in range(layers):
            pltpu.make_async_copy(zero_ref, out_ref.at[l, j], sems.at[l, j]).wait()
        return carry

    lax.fori_loop(0, slots, done, 0)


def mix_kernel(n_parts, n_cut, *refs):
    parts, refs = refs[:n_parts], refs[n_parts:]
    order_ref, w_ref, own_ref, refs = refs[0], refs[1], refs[2], refs[3:]
    pieces, out_ref = refs[:-1], refs[-1]
    halves, shards, depth, _ = w_ref.shape

    def dot(a, b):
        return jnp.dot(a, b, preferred_element_type=jnp.float32)

    gathered = pl.program_id(0) < pl.num_programs(0) // 2

    @pl.when(gathered)
    def _():
        total = jnp.zeros(out_ref.shape, jnp.float32)
        for k, part in enumerate(parts):
            for half in range(halves):
                cut = part[:, half * depth : (half + 1) * depth]
                total = total + dot(cut, w_ref[half, order_ref[k]])
        out_ref[...] = total.astype(jnp.bfloat16)

    @pl.when(jnp.logical_not(gathered))
    def _():
        total = dot(parts[-1][...], own_ref[...])
        for k in range(n_parts - 1):
            for c in range(n_cut):
                piece = pieces[k * n_cut + c]
                rows = piece.shape[0]
                at = pl.multiple_of(order_ref[n_parts + c] * rows, rows)
                total = total + dot(parts[k][:, pl.ds(at, rows)], piece[...])
        out_ref[...] = total.astype(jnp.bfloat16)


def mix(parts, order, w_all, w_out, pieces, n_cut):
    rows, depth = parts[0].shape
    halves, shards, half_depth, _ = w_all.shape
    width = w_out.shape[1]
    tile = 512
    tiles = width // tile
    first = tiles // 2
    part = pl.BlockSpec((rows, depth), lambda i: (0, 0))
    piece = pl.BlockSpec((pieces[0].shape[0], tile), lambda i: (0, jnp.maximum(i - first, 0)))
    return pl.pallas_call(
        functools.partial(mix_kernel, len(parts), n_cut),
        grid=(tiles,),
        in_specs=[part] * len(parts)
        + [
            pl.BlockSpec(memory_space=pltpu.SMEM),
            pl.BlockSpec(
                (halves, shards, half_depth, tile), lambda i: (0, 0, 0, jnp.minimum(i, first - 1))
            ),
            pl.BlockSpec((depth, tile), lambda i: (0, jnp.maximum(i, first))),
        ]
        + [piece] * len(pieces),
        out_specs=pl.BlockSpec((rows, tile), lambda i: (0, i)),
        out_shape=jax.ShapeDtypeStruct((rows, width), jnp.bfloat16),
        compiler_params=pltpu.CompilerParams(vmem_limit_bytes=VMEM_LIMIT),
        cost_estimate=pl.CostEstimate(
            flops=2 * rows * depth * 4 * width, bytes_accessed=10**7, transcendentals=0
        ),
        name="mix",
    )(*parts, order, w_all, w_out, *pieces)


def per_device(tokens, norm_gain, w_query, w_keyval, w_out, kv_cache, lengths, dest_slot):
    prompts = lengths.shape[0]
    fresh_rows = tokens.shape[0] // prompts
    layers, _, blocks_win, block_len, lane_width = kv_cache.shape
    per_dev = prompts * blocks_win
    devices = lax.axis_size(("group", "dp"))
    capacity = per_dev // devices // 2
    total = devices * capacity
    me = lax.axis_index(("group", "dp")).astype(jnp.int32)
    dest_flat = dest_slot.reshape(-1)
    raw = kv_cache.reshape(layers, per_dev, block_len, lane_width)

    smem = pl.BlockSpec(memory_space=pltpu.SMEM)
    hbm = pl.BlockSpec(memory_space=pltpu.HBM)
    rows = layers * block_len + 16
    outgoing = pl.pallas_call(
        pick_kernel,
        in_specs=[smem, smem, smem, hbm],
        out_specs=pl.BlockSpec(memory_space=pltpu.VMEM),
        out_shape=jax.ShapeDtypeStruct((total, rows, lane_width), jnp.bfloat16),
        scratch_shapes=[
            pltpu.SMEM((devices,), jnp.int32),
            pltpu.SemaphoreType.DMA((total, layers)),
        ],
        compiler_params=pltpu.CompilerParams(vmem_limit_bytes=VMEM_LIMIT),
        cost_estimate=pl.CostEstimate(flops=0, bytes_accessed=10**7, transcendentals=0),
        name="pick",
    )(me.reshape(1), dest_flat, lengths, raw)
    norm_gain, outgoing = lax.optimization_barrier((norm_gain, outgoing))
    incoming = lax.all_to_all(outgoing, ("group", "dp"), split_axis=0, concat_axis=0, tiled=True)

    t_size = lax.axis_size("tensor")

    def shift(by):
        return [(i, (i + by) % t_size) for i in range(t_size)]

    cores = lax.axis_size("dp")
    core = lax.axis_index("dp").astype(jnp.int32)
    depth = w_out.shape[0] // cores
    split = w_out.shape[1] // 2
    half = lax.dynamic_slice(w_out, (core * depth, 0), (depth, split))
    w_all = lax.all_gather(half, ("dp", "tensor"), axis=0).reshape(cores, -1, *half.shape)
    if cores == 2:
        mine = lax.dynamic_slice(w_out, (core * depth, split), (depth, split))
        places = [core, 1 - core]
    else:
        mine = w_out[:, split:]
        places = [jnp.zeros((), jnp.int32)]
    sent = [lax.ppermute(mine, "tensor", shift(step)) for step in range(1, t_size)]

    query, keyval = project(tokens, norm_gain, w_query, w_keyval, fresh_rows)
    t = lax.axis_index("tensor").astype(jnp.int32)
    parts, order = [], []
    for step in range(1, t_size + 1):
        p = (t + step) % t_size
        own = lax.dynamic_index_in_dim(lengths, p, 0, keepdims=False)
        info = jnp.concatenate([p.reshape(1), own])
        if step > 1:
            info = lax.optimization_barrier((info, part))[0]
        if step == t_size and cores == 2:
            info, *sent = lax.optimization_barrier((info, *sent))
            swapped = [lax.ppermute(piece, "dp", [(0, 1), (1, 0)]) for piece in sent]
            sent = [piece for pair in zip(sent, swapped) for piece in pair]
        part = attend(info, query, keyval, kv_cache)
        parts.append(lax.ppermute(part, "tensor", shift(step)) if step < t_size else part)
        order.append((t - step + t_size) % t_size)
    mixed = mix(parts, jnp.stack(order + places), w_all, w_out, sent, len(places))

    slots = incoming[:, layers * block_len, 0].astype(jnp.int32)
    decode_cache = pl.pallas_call(
        place_kernel,
        in_specs=[smem, hbm],
        out_specs=hbm,
        out_shape=jax.ShapeDtypeStruct((layers, per_dev, block_len, lane_width), jnp.bfloat16),
        scratch_shapes=[
            pltpu.SMEM((per_dev,), jnp.int32),
            pltpu.VMEM((block_len, lane_width), jnp.bfloat16),
            pltpu.VMEM((total, rows, lane_width), jnp.bfloat16),
            pltpu.SemaphoreType.DMA,
            pltpu.SemaphoreType.DMA((layers, per_dev)),
        ],
        compiler_params=pltpu.CompilerParams(vmem_limit_bytes=VMEM_LIMIT),
        cost_estimate=pl.CostEstimate(flops=0, bytes_accessed=10**7, transcendentals=0),
        name="place",
    )(slots, lax.optimization_barrier((incoming, part))[0])
    return (mixed, decode_cache)


def solution(mesh):
    in_specs = (
        P(("group", "dp"), None),
        P(),
        P(None, "tensor"),
        P(None, "tensor"),
        P("tensor", None),
        P(None, ("group", "dp"), None, None, "tensor"),
        P(("group", "dp"), None),
        P(),
    )
    out_specs = (P(("group", "dp", "tensor"), None), P(None, ("group", "dp"), None, "tensor"))
    return jax.shard_map(
        per_device, mesh=mesh, in_specs=in_specs, out_specs=out_specs, check_vma=False
    )
```
